32 devices in a mesh: orow: 8 (over z, x), ocol: 4 (over y, core).
Axes of the slice: x: 2, y: 2, z: 4, core: 2. Of those that a mesh axis runs over, the one named last changes fastest.
Arguments:
- integrals: bfloat16 [2304, 16, 384], P('ocol', 'orow'), may hold values from -0.29882812 to 0.29882812
- occ_count: int32 [8], replicated, may hold values from 1 to 2
- occ_energy: float32 [16], replicated, may hold values from -2 to -0.5
- vir_energy: float32 [384], replicated, may hold values from 0.3 to 2.5
- task_iblock: int32 [32, 1], replicated, may hold values from 0 to 7; in each aligned block of 32 rows (0 to 31, 32 to 63, ...) at most 8 rows name the same one
- task_jblock: int32 [32], replicated, may hold values from 0 to 7
Outputs:
- gamma_out: float32 [2304, 16, 384], P('ocol', 'orow')
- density: float32 [384, 384], replicated
The draws below stay inside these ranges and needn't reach their ends.
Inputs may be any that keep to these rules, and one draw needn't show every extreme that they name: `task_iblock`: no first block is named by more than 8 tasks, and some first block by exactly 8.
All inputs are finite; a program needn't handle non-finite values.
Results may differ from the reference program's by a relative error of at most 0.0019.
Values may be sent and summed in bfloat16 or wider, within the bound.
A program may use at most 128 MiB of HBM per device.

```python
import math
import jax
import jax.numpy as jnp
import numpy as np
from jax import lax

NAUX = 2304
NVIR = 384
OB = 2
MOST = 8
TASKS = 32
OCC = 16
N_OROW = 8


def with_ends(result, stream_key, least, largest):
    extent = result.shape
    index_at = [jax.random.randint(jax.random.fold_in(stream_key, axis), (), 0, extent[axis]) for axis in range(len(extent))]
    result = result.at[tuple(index_at)].set(least)
    longest = extent.index(max(extent))
    index_at[longest] = (index_at[longest] + 1) % extent[longest]
    return result.at[tuple(index_at)].set(largest)


def block_levels(rng, dims, shards, low, top_value):
    loudness = 1.0
    for position, parts in shards:
        heights = jax.random.uniform(jax.random.fold_in(jax.random.fold_in(rng, 6), position), (parts,), jnp.float32, low / len(shards), top_value / len(shards))
        loudness = loudness * jnp.repeat(jnp.exp(heights), dims[position] // parts).reshape((-1,) + (1,) * (len(dims) - 1 - position))
    return loudness


def deal_out(rng, own, number, rows, count, top, reach, skew):
    order = jax.random.permutation(rng, count)
    crowded, ordinary = shares(count, rows * top, reach, skew, True), shares(count, rows * top, reach, skew, False)
    places = jnp.arange(count)

    def named(tallies, turn):
        used = int((tallies > 0).sum())
        fixed = max(1, used // 4)
        shifted = fixed + (places - fixed + turn * (used - fixed)) % max(1, count - fixed)
        return jnp.zeros((count,), jnp.int32).at[order[jnp.where(places < fixed, places, shifted)]].set(jnp.asarray(tallies, jnp.int32))

    tallies = jnp.where(number % 4 == 0, named(crowded, number // 4), named(ordinary, number - number // 4 - 1))
    mixed = jax.random.permutation(jax.random.fold_in(own, 3), count)
    source_of, taker = mixed[0:count // 2 * 2:2], mixed[1:count // 2 * 2:2]
    slack = jnp.minimum(tallies[source_of] - 1, reach - tallies[taker]) // 2
    slack = jnp.where((source_of == order[0]) | (taker == order[0]) | (tallies[taker] == 0), 0, jnp.maximum(slack, 0))
    shifted = jax.random.randint(jax.random.fold_in(own, 4), (count // 2,), 0, 1 << 20) % (slack + 1)
    tallies = tallies.at[source_of].add(-shifted).at[taker].add(shifted)
    items = jnp.searchsorted(jnp.cumsum(tallies), jnp.arange(rows * top), side="right").astype(jnp.int32)
    table = items.reshape(top, rows).T
    table = table[jax.random.permutation(jax.random.fold_in(own, 1), rows)]
    turn = jax.random.randint(jax.random.fold_in(own, 2), (rows, 1), 0, top)
    return jnp.take_along_axis(table, (jnp.arange(top)[None, :] + turn) % top, axis=1)


def shares(amount, total, most, lean, full):
    portions = [(1 << 20) // math.isqrt(grade ** lean) + 1 for grade in range(1, amount + 1)]
    largest = most if full else min(most, max(-(-total // amount), total * portions[0] // sum(portions)))
    least = 1 if total - largest >= amount - 1 else 0
    given, surplus = [largest] + [least] * (amount - 1), total - largest - least * (amount - 1)
    while surplus > 0:
        movable = [i for i in range(1, amount) if given[i] < largest] or [i for i in range(1, amount) if given[i] < most]
        pool, left = sum([portions[i] for i in movable]), surplus
        for i in movable:
            more = min(most - given[i], max(1, left * portions[i] // pool), surplus)
            given[i] = given[i] + more
            surplus = surplus - more
    return np.array(given)


def centred(stream_key, dims, scale, bound, pieces=(), kind=jnp.bfloat16):
    result = scale * jax.random.normal(stream_key, dims, jnp.float32)
    if pieces:
        result = result * block_levels(stream_key, dims, pieces, -0.22, 0.18)
    return jnp.clip(result, -bound, bound).astype(kind)


def setup_inputs(seed: int = 0) -> dict:
    key_list = jax.random.split(jax.random.key(seed), 7)
    integrals = centred(key_list[0], (NAUX, OCC, NVIR), 0.05, 0.29882812, ((0, 4), (1, 8)))
    occ_count = with_ends(jax.random.randint(key_list[1], (N_OROW,), 1, OB + 1), jax.random.fold_in(key_list[1], 1), 1, OB).astype(jnp.int32)
    occ_energy = jnp.clip(jax.random.uniform(key_list[2], (OCC,), jnp.float32, -2.0, -0.5), -2.0, -0.5)
    vir_energy = jnp.clip(jax.random.uniform(key_list[3], (NVIR,), jnp.float32, 0.3, 2.5), 0.3, 2.5)
    task_iblock_keys = jax.random.split(jax.random.fold_in(key_list[4], 1), TASKS // TASKS)
    task_iblock_turns = jax.random.permutation(jax.random.fold_in(key_list[4], 3), TASKS // TASKS)
    task_iblock = jax.vmap(lambda own, number: deal_out(jax.random.fold_in(key_list[4], 2), own, number, TASKS, N_OROW, 1, MOST, 2))(task_iblock_keys, task_iblock_turns).reshape((TASKS, 1))
    task_jblock = with_ends(jax.random.randint(key_list[5], (TASKS,), 0, N_OROW), jax.random.fold_in(key_list[5], 1), 0, N_OROW - 1).astype(jnp.int32)
    return {"integrals": integrals, "occ_count": occ_count, "occ_energy": occ_energy, "vir_energy": vir_energy, "task_iblock": task_iblock, "task_jblock": task_jblock}


def amplitude(k_total, i_energy, j_energy, vir_energy):
    orbitals = i_energy.shape[0]
    virtuals = vir_energy.shape[0]
    k_grid = k_total.reshape(orbitals, virtuals, orbitals, virtuals)
    denominator = (i_energy[:, None, None, None] + j_energy[None, None, :, None]
                   - vir_energy[None, :, None, None] - vir_energy[None, None, None, :])
    values = (2.0 * k_grid - jnp.swapaxes(k_grid, 1, 3)) / denominator
    return values.reshape(orbitals * virtuals, orbitals * virtuals)


def reference(integrals, occ_count, occ_energy, vir_energy, task_iblock, task_jblock):
    orbital_ids = jnp.arange(OCC, dtype=jnp.int32)
    active = (orbital_ids % OB) < occ_count[orbital_ids // OB]
    masked = integrals * active.astype(jnp.bfloat16)[None, :, None]
    flat_blocks = masked.reshape(NAUX, N_OROW, OB * NVIR)
    energy_grid = occ_energy.reshape(N_OROW, OB)

    def step(carry, pair):
        gamma_sum, dens_sum = carry
        first, second = pair
        i_rows = lax.dynamic_index_in_dim(flat_blocks, first, 1, keepdims=False)
        j_rows = lax.dynamic_index_in_dim(flat_blocks, second, 1, keepdims=False)
        k_total = jnp.dot(i_rows.T, j_rows, preferred_element_type=jnp.float32)
        i_energy = lax.dynamic_index_in_dim(energy_grid, first, 0, keepdims=False)
        j_energy = lax.dynamic_index_in_dim(energy_grid, second, 0, keepdims=False)
        amplitudes = amplitude(k_total, i_energy, j_energy, vir_energy).astype(jnp.bfloat16)
        gamma_i = jnp.dot(j_rows, amplitudes.T, preferred_element_type=jnp.float32)
        gamma_j = jnp.dot(i_rows, amplitudes, preferred_element_type=jnp.float32)
        gamma_sum = gamma_sum.at[:, first].add(gamma_i).at[:, second].add(gamma_j)
        grid = amplitudes.astype(jnp.float32).reshape(OB, NVIR, OB * NVIR)
        dens_sum = dens_sum + jnp.einsum('iaw,ibw->ab', grid, grid)
        return (gamma_sum, dens_sum), None

    start = (jnp.zeros((NAUX, N_OROW, OB * NVIR), jnp.float32), jnp.zeros((NVIR, NVIR), jnp.float32))
    pairs = (task_iblock[:, 0].astype(jnp.int32), task_jblock.astype(jnp.int32))
    (gamma_sum, dens_sum), _ = lax.scan(step, start, pairs)
    gamma_out = gamma_sum.reshape(NAUX, OCC, NVIR)
    density = dens_sum / TASKS
    return gamma_out, density
```

```python
import functools

import jax
import jax.numpy as jnp
from jax import lax
from jax.experimental import pallas as pl
from jax.experimental.pallas import tpu as pltpu
from jax.sharding import PartitionSpec as P


def pair_kernel(orbitals, cols, num_ref, occ_ref, gr_ref, gs_ref, gc_ref, vrow_ref, vcol_ref, gamma_ref, dens_ref, flip_ref):
    s = pl.program_id(0)
    blocks = pl.num_programs(0)
    row, col = num_ref[0], num_ref[1]
    virtuals = vrow_ref.shape[1]

    @pl.when(s == 0)
    def _():
        gamma_ref[...] = jnp.zeros_like(gamma_ref)
        dens_ref[...] = jnp.zeros_like(dens_ref)
        flip_ref[...] = gr_ref[0].T

    touch = num_ref[2 + s]
    first = num_ref[2 + blocks + s]

    @pl.when(touch > 0)
    def _():
        weight = touch.astype(jnp.float32)
        for i in range(orbitals):
            own = pl.ds(i * virtuals, virtuals)
            k_rows = jnp.dot(flip_ref[own, :], gs_ref[0], preferred_element_type=jnp.float32)
            parts = []
            for j in range(orbitals):
                k_ij = k_rows[:, j * virtuals:(j + 1) * virtuals]
                pair = occ_ref[row * orbitals + i] + occ_ref[s * orbitals + j]
                denominator = (pair - vcol_ref[...]) - vrow_ref[...]
                parts.append(((2.0 * k_ij - k_ij.T) / denominator).astype(jnp.bfloat16))
            amp = jnp.concatenate(parts, axis=1)
            gamma_ref[:, own] += weight * lax.dot_general(
                gc_ref[0], amp, (((1,), (1,)), ((), ())), preferred_element_type=jnp.float32)

            @pl.when((first > 0) & (lax.rem(s, cols) == col))
            def _():
                dens_ref[...] += first.astype(jnp.float32) * lax.dot_general(
                    amp, amp, (((1,), (1,)), ((), ())), preferred_element_type=jnp.float32)


def local(integrals, occ_count, occ_energy, vir_energy, task_iblock, task_jblock):
    aux_local, orbitals, virtuals = integrals.shape
    span = orbitals * virtuals
    blocks = lax.axis_size("orow")
    cols = lax.axis_size("ocol")
    row = lax.axis_index("orow")
    col = lax.axis_index("ocol")
    aux = aux_local * cols
    active = jnp.arange(orbitals) < occ_count[row]
    masked = integrals * active.astype(jnp.bfloat16)[None, :, None]
    shard = masked.reshape(aux_local, span)
    gathered = lax.all_gather(shard, ("orow", "ocol"), axis=0, tiled=True).reshape(blocks, aux, span)
    i_list, j_list = task_iblock[:, 0], task_jblock
    ids = jnp.arange(blocks)
    i_hot = i_list[None, :] == ids[:, None]
    j_hot = j_list[None, :] == ids[:, None]
    first = jnp.sum((i_list == row)[None, :] & j_hot, axis=1).astype(jnp.int32)
    second = jnp.sum((j_list == row)[None, :] & i_hot, axis=1).astype(jnp.int32)
    numbers = jnp.concatenate([jnp.stack([row, col]).astype(jnp.int32), first + second, first])
    gamma, dens = pl.pallas_call(
        functools.partial(pair_kernel, orbitals, cols),
        grid_spec=pltpu.PrefetchScalarGridSpec(
            num_scalar_prefetch=2,
            grid=(blocks,),
            in_specs=[
                pl.BlockSpec((1, aux, span), lambda s, num, occ: (num[0], 0, 0)),
                pl.BlockSpec((1, aux, span), lambda s, num, occ: (s, 0, 0)),
                pl.BlockSpec((1, aux_local, span), lambda s, num, occ: (s, num[1], 0)),
                pl.BlockSpec((1, virtuals), lambda s, num, occ: (0, 0)),
                pl.BlockSpec((virtuals, 1), lambda s, num, occ: (0, 0)),
            ],
            out_specs=[
                pl.BlockSpec((aux_local, span), lambda s, num, occ: (0, 0)),
                pl.BlockSpec((virtuals, virtuals), lambda s, num, occ: (0, 0)),
            ],
            scratch_shapes=[pltpu.VMEM((span, aux), jnp.bfloat16)],
        ),
        out_shape=[
            jax.ShapeDtypeStruct((aux_local, span), jnp.float32),
            jax.ShapeDtypeStruct((virtuals, virtuals), jnp.float32),
        ],
        compiler_params=pltpu.CompilerParams(vmem_limit_bytes=56 * 1024 * 1024),
    )(numbers, occ_energy, gathered, gathered, gathered, vir_energy[None, :], vir_energy[:, None])
    density = lax.psum(dens, ("orow", "ocol")) / i_list.shape[0]
    return gamma.reshape(aux_local, orbitals, virtuals), density


def solution(mesh):
    return jax.shard_map(
        local,
        mesh=mesh,
        in_specs=(P("ocol", "orow", None), P(), P(), P(), P(), P()),
        out_specs=(P("ocol", "orow", None), P()),
        check_vma=False,
    )
```

```python
import functools

import jax
import jax.numpy as jnp
from jax import lax
from jax.experimental import pallas as pl
from jax.experimental.pallas import tpu as pltpu
from jax.sharding import PartitionSpec as P

MESH = pl.DeviceIdType.MESH


def pair_kernel(orbitals, cols, num_ref, occ_ref, gr_ref, gs_ref, gc_ref, vrow_ref, vcol_ref, gamma_ref, dens_ref, flip_ref, amp_ref):
    s = pl.program_id(0)
    blocks = pl.num_programs(0)
    row, col = num_ref[0], num_ref[1]
    virtuals = vrow_ref.shape[1]

    @pl.when(s == 0)
    def _():
        gamma_ref[...] = jnp.zeros_like(gamma_ref)
        dens_ref[...] = jnp.zeros_like(dens_ref)
        flip_ref[...] = gr_ref[0].T

    touch = num_ref[2 + s]
    first = num_ref[2 + blocks + s]

    @pl.when(touch > 0)
    def _():
        weight = touch.astype(jnp.float32)
        for i in range(orbitals):
            own = pl.ds(i * virtuals, virtuals)
            k_rows = jnp.dot(flip_ref[own, :], gs_ref[0], preferred_element_type=jnp.float32)
            parts = []
            for j in range(orbitals):
                k_ij = k_rows[:, j * virtuals:(j + 1) * virtuals]
                pair = occ_ref[row * orbitals + i] + occ_ref[s * orbitals + j]
                denominator = (pair - vcol_ref[...]) - vrow_ref[...]
                parts.append(((2.0 * k_ij - k_ij.T) / denominator).astype(jnp.bfloat16))
            amp = jnp.concatenate(parts, axis=1)
            amp_ref[...] = amp
            gamma_ref[:, own] += weight * lax.dot_general(
                gc_ref[0], amp, (((1,), (1,)), ((), ())), preferred_element_type=jnp.float32)

            @pl.when(first > 0)
            def _():
                strip = virtuals // cols
                mine = amp_ref[pl.ds(pl.multiple_of(col * strip, strip), strip), :]
                dens_ref[...] += first.astype(jnp.float32) * lax.dot_general(
                    mine, amp_ref[...], (((1,), (1,)), ((), ())), preferred_element_type=jnp.float32)


def density_kernel(scale, part_ref, out_ref, arrived, send_sem, take_sem, pass_sem, row_sem, fan_sem, col_sem):
    rows, cols = lax.axis_size("orow"), lax.axis_size("ocol")
    row, col = lax.axis_index("orow"), lax.axis_index("ocol")
    barrier = pltpu.get_barrier_semaphore()

    def peer(step):
        return lax.rem(row + step, rows)

    def other(step):
        return lax.rem(col + step, cols)

    @pl.loop(1, rows)
    def _(step):
        pl.semaphore_signal(barrier, inc=1, device_id={"orow": peer(step)}, device_id_type=MESH)

    @pl.loop(1, cols)
    def _(step):
        pl.semaphore_signal(barrier, inc=1, device_id={"ocol": other(step)}, device_id_type=MESH)

    pl.semaphore_wait(barrier, rows + cols - 2)

    def scatter(step):
        return pltpu.make_async_remote_copy(
            src_ref=part_ref.at[peer(step)], dst_ref=arrived.at[step - 1], send_sem=send_sem.at[step - 1],
            recv_sem=take_sem.at[step - 1], device_id={"orow": peer(step)}, device_id_type=MESH)

    def spread(step):
        spot = out_ref.at[col, row]
        return pltpu.make_async_remote_copy(
            src_ref=spot, dst_ref=spot, send_sem=pass_sem.at[step - 1],
            recv_sem=row_sem.at[step - 1], device_id={"orow": peer(step)}, device_id_type=MESH)

    def fan(step):
        spot = out_ref.at[col]
        return pltpu.make_async_remote_copy(
            src_ref=spot, dst_ref=spot, send_sem=fan_sem.at[step - 1],
            recv_sem=col_sem.at[step - 1], device_id={"ocol": other(step)}, device_id_type=MESH)

    @pl.loop(1, rows)
    def _(step):
        scatter(step).start()

    total = part_ref[row]
    for step in range(1, rows):
        scatter(step).wait()
        total = total + arrived[step - 1]
    out_ref[col, row] = total * scale

    @pl.loop(1, rows)
    def _(step):
        spread(step).start()

    @pl.loop(1, rows)
    def _(step):
        spread(step).wait()

    @pl.loop(1, cols)
    def _(step):
        fan(step).start()

    @pl.loop(1, cols)
    def _(step):
        fan(step).wait()


def sum_density(part, tasks):
    rows, cols = lax.axis_size("orow"), lax.axis_size("ocol")
    strip, virtuals = part.shape
    share = strip // rows
    full = pl.pallas_call(
        functools.partial(density_kernel, 1.0 / tasks),
        out_shape=jax.ShapeDtypeStruct((cols, rows, share, virtuals), jnp.float32),
        in_specs=[pl.BlockSpec(memory_space=pltpu.VMEM)],
        out_specs=pl.BlockSpec(memory_space=pltpu.VMEM),
        scratch_shapes=[
            pltpu.VMEM((rows - 1, share, virtuals), jnp.float32),
            pltpu.SemaphoreType.DMA((rows - 1,)),
            pltpu.SemaphoreType.DMA((rows - 1,)),
            pltpu.SemaphoreType.DMA((rows - 1,)),
            pltpu.SemaphoreType.DMA((rows - 1,)),
            pltpu.SemaphoreType.DMA((cols - 1,)),
            pltpu.SemaphoreType.DMA((cols - 1,)),
        ],
        compiler_params=pltpu.CompilerParams(collective_id=1, has_side_effects=True),
    )(part.reshape(rows, share, virtuals))
    return full.reshape(virtuals, virtuals)


def local(integrals, occ_count, occ_energy, vir_energy, task_iblock, task_jblock):
    aux_local, orbitals, virtuals = integrals.shape
    span = orbitals * virtuals
    blocks = lax.axis_size("orow")
    cols = lax.axis_size("ocol")
    row = lax.axis_index("orow")
    col = lax.axis_index("ocol")
    aux = aux_local * cols
    active = jnp.arange(orbitals) < occ_count[row]
    masked = integrals * active.astype(jnp.bfloat16)[None, :, None]
    shard = masked.reshape(aux_local, span)
    gathered = lax.all_gather(shard, ("orow", "ocol"), axis=0, tiled=True).reshape(blocks, aux, span)
    i_list, j_list = task_iblock[:, 0], task_jblock
    ids = jnp.arange(blocks)
    i_hot = i_list[None, :] == ids[:, None]
    j_hot = j_list[None, :] == ids[:, None]
    first = jnp.sum((i_list == row)[None, :] & j_hot, axis=1).astype(jnp.int32)
    second = jnp.sum((j_list == row)[None, :] & i_hot, axis=1).astype(jnp.int32)
    numbers = jnp.concatenate([jnp.stack([row, col]).astype(jnp.int32), first + second, first])
    gamma, dens = pl.pallas_call(
        functools.partial(pair_kernel, orbitals, cols),
        grid_spec=pltpu.PrefetchScalarGridSpec(
            num_scalar_prefetch=2,
            grid=(blocks,),
            in_specs=[
                pl.BlockSpec((1, aux, span), lambda s, num, occ: (num[0], 0, 0)),
                pl.BlockSpec((1, aux, span), lambda s, num, occ: (s, 0, 0)),
                pl.BlockSpec((1, aux_local, span), lambda s, num, occ: (s, num[1], 0)),
                pl.BlockSpec((1, virtuals), lambda s, num, occ: (0, 0)),
                pl.BlockSpec((virtuals, 1), lambda s, num, occ: (0, 0)),
            ],
            out_specs=[
                pl.BlockSpec((aux_local, span), lambda s, num, occ: (0, 0)),
                pl.BlockSpec((virtuals // cols, virtuals), lambda s, num, occ: (0, 0)),
            ],
            scratch_shapes=[pltpu.VMEM((span, aux), jnp.bfloat16), pltpu.VMEM((virtuals, span), jnp.bfloat16)],
        ),
        out_shape=[
            jax.ShapeDtypeStruct((aux_local, span), jnp.float32),
            jax.ShapeDtypeStruct((virtuals // cols, virtuals), jnp.float32),
        ],
        compiler_params=pltpu.CompilerParams(vmem_limit_bytes=56 * 1024 * 1024),
    )(numbers, occ_energy, gathered, gathered, gathered, vir_energy[None, :], vir_energy[:, None])
    density = sum_density(dens, i_list.shape[0])
    return gamma.reshape(aux_local, orbitals, virtuals), density


def solution(mesh):
    return jax.shard_map(
        local,
        mesh=mesh,
        in_specs=(P("ocol", "orow", None), P(), P(), P(), P(), P()),
        out_specs=(P("ocol", "orow", None), P()),
        check_vma=False,
    )
```

```python
import functools

import jax
import jax.numpy as jnp
from jax import lax
from jax.experimental import pallas as pl
from jax.experimental.pallas import tpu as pltpu
from jax.sharding import PartitionSpec as P

MESH = pl.DeviceIdType.MESH


def pair_kernel(orbitals, cols, num_ref, occ_ref, gr_ref, gs_ref, gc_ref, vrow_ref, vcol_ref, gamma_ref, dens_ref, flip_ref, amp_ref):
    s = pl.program_id(0)
    blocks = pl.num_programs(0)
    row, col = num_ref[0], num_ref[1]
    virtuals = vrow_ref.shape[1]

    @pl.when(s == 0)
    def _():
        gamma_ref[...] = jnp.zeros_like(gamma_ref)
        dens_ref[...] = jnp.zeros_like(dens_ref)
        flip_ref[...] = gr_ref[0].T

    touch = num_ref[2 + s]
    first = num_ref[2 + blocks + s]

    @pl.when(touch > 0)
    def _():
        weight = touch.astype(jnp.float32)
        for i in range(orbitals):
            own = pl.ds(i * virtuals, virtuals)
            k_rows = jnp.dot(flip_ref[own, :], gs_ref[0], preferred_element_type=jnp.float32)
            parts = []
            for j in range(orbitals):
                k_ij = k_rows[:, j * virtuals:(j + 1) * virtuals]
                pair = occ_ref[row * orbitals + i] + occ_ref[s * orbitals + j]
                denominator = (pair - vcol_ref[...]) - vrow_ref[...]
                parts.append(((2.0 * k_ij - k_ij.T) / denominator).astype(jnp.bfloat16))
            amp = jnp.concatenate(parts, axis=1)
            amp_ref[...] = amp
            gamma_ref[:, own] += weight * lax.dot_general(
                gc_ref[0], amp, (((1,), (1,)), ((), ())), preferred_element_type=jnp.float32)

            @pl.when(first > 0)
            def _():
                strip = virtuals // cols
                mine = amp_ref[pl.ds(pl.multiple_of(col * strip, strip), strip), :]
                dens_ref[...] += first.astype(jnp.float32) * lax.dot_general(
                    mine, amp_ref[...], (((1,), (1,)), ((), ())), preferred_element_type=jnp.float32)


def density_kernel(scale, part_ref, out_ref, arrived, send_sem, take_sem, pass_sem, row_sem, fan_sem, col_sem):
    rows, cols = lax.axis_size("orow"), lax.axis_size("ocol")
    row, col = lax.axis_index("orow"), lax.axis_index("ocol")
    barrier = pltpu.get_barrier_semaphore()

    def peer(step):
        return lax.rem(row + step, rows)

    def other(step):
        return lax.rem(col + step, cols)

    @pl.loop(1, rows)
    def _(step):
        pl.semaphore_signal(barrier, inc=1, device_id={"orow": peer(step)}, device_id_type=MESH)

    @pl.loop(1, cols)
    def _(step):
        pl.semaphore_signal(barrier, inc=1, device_id={"ocol": other(step)}, device_id_type=MESH)

    pl.semaphore_wait(barrier, rows + cols - 2)

    def scatter(step):
        return pltpu.make_async_remote_copy(
            src_ref=part_ref.at[peer(step)], dst_ref=arrived.at[step - 1], send_sem=send_sem.at[step - 1],
            recv_sem=take_sem.at[step - 1], device_id={"orow": peer(step)}, device_id_type=MESH)

    def spread(step):
        spot = out_ref.at[col, row]
        return pltpu.make_async_remote_copy(
            src_ref=spot, dst_ref=spot, send_sem=pass_sem.at[step - 1],
            recv_sem=row_sem.at[step - 1], device_id={"orow": peer(step)}, device_id_type=MESH)

    def fan(step):
        spot = out_ref.at[col]
        return pltpu.make_async_remote_copy(
            src_ref=spot, dst_ref=spot, send_sem=fan_sem.at[step - 1],
            recv_sem=col_sem.at[step - 1], device_id={"ocol": other(step)}, device_id_type=MESH)

    @pl.loop(1, rows)
    def _(step):
        scatter(step).start()

    total = part_ref[row]
    for step in range(1, rows):
        scatter(step).wait()
        total = total + arrived[step - 1]
    out_ref[col, row] = total * scale

    @pl.loop(1, rows)
    def _(step):
        spread(step).start()

    @pl.loop(1, rows)
    def _(step):
        spread(step).wait()

    @pl.loop(1, cols)
    def _(step):
        fan(step).start()

    @pl.loop(1, cols)
    def _(step):
        fan(step).wait()


def sum_density(part, tasks):
    rows, cols = lax.axis_size("orow"), lax.axis_size("ocol")
    strip, virtuals = part.shape
    share = strip // rows
    full = pl.pallas_call(
        functools.partial(density_kernel, 1.0 / tasks),
        out_shape=jax.ShapeDtypeStruct((cols, rows, share, virtuals), jnp.float32),
        in_specs=[pl.BlockSpec(memory_space=pltpu.VMEM)],
        out_specs=pl.BlockSpec(memory_space=pltpu.VMEM),
        scratch_shapes=[
            pltpu.VMEM((rows - 1, share, virtuals), jnp.float32),
            pltpu.SemaphoreType.DMA((rows - 1,)),
            pltpu.SemaphoreType.DMA((rows - 1,)),
            pltpu.SemaphoreType.DMA((rows - 1,)),
            pltpu.SemaphoreType.DMA((rows - 1,)),
            pltpu.SemaphoreType.DMA((cols - 1,)),
            pltpu.SemaphoreType.DMA((cols - 1,)),
        ],
        compiler_params=pltpu.CompilerParams(collective_id=1, has_side_effects=True),
    )(part.reshape(rows, share, virtuals))
    return full.reshape(virtuals, virtuals)


def gather_kernel(nz, nx, ny, cut, shard_ref, all_ref, own_sem, send_sem, line_sem, pair_sem):
    aux_local = shard_ref.shape[0]
    row, col = lax.axis_index("orow"), lax.axis_index("ocol")
    z, x, y, k = row // nx, lax.rem(row, nx), col // 2, lax.rem(col, 2)
    spans = (pl.ds(0, cut), pl.ds(cut, aux_local - cut))

    def turn(at, by, extent):
        return lax.rem(at + by, extent)

    def place(dz=0, dx=0, dy=0):
        return turn(z, dz, nz) * nx + turn(x, dx, nx), turn(y, dy, ny)

    def device(dz=0, dx=0, dy=0, dk=0):
        r, c = place(dz, dx, dy)
        return {"orow": r, "ocol": c * 2 + lax.rem(k + dk, 2)}

    near = sorted(range(1, nz), key=lambda d: min(d, nz - d))
    lines = {
        "z": [dict(dz=d) for d in near],
        "x": [dict(dx=d) for d in range(1, nx)],
        "y": [dict(dy=d) for d in range(1, ny)],
    }
    peers = lines["z"] + lines["x"] + lines["y"] + [dict(dk=1)]
    barrier = pltpu.get_barrier_semaphore()
    for peer in peers:
        pl.semaphore_signal(barrier, inc=1, device_id=device(**peer), device_id_type=MESH)
    pl.semaphore_wait(barrier, len(peers))

    sent = []

    def push(piece, at, source, sem, peer):
        r, c = place(**at)
        copy = pltpu.make_async_remote_copy(
            src_ref=source, dst_ref=all_ref.at[r, c * 2 + k, spans[piece]], send_sem=send_sem.at[len(sent)],
            recv_sem=sem, device_id=device(**peer), device_id_type=MESH)
        copy.start()
        sent.append(copy)

    def pass_on(piece, at, order):
        r, c = place(**at)
        own = not at
        source = shard_ref.at[spans[piece]] if own else all_ref.at[r, c * 2 + k, spans[piece]]
        for axis in order:
            for peer in lines[axis]:
                push(piece, at, source, line_sem.at[piece, r, c], peer)
        push(piece, at, source, pair_sem.at[piece, r, c], dict(dk=1))

    def take(piece, at, sem, core):
        r, c = place(**at)
        spot = all_ref.at[r, c * 2 + core, spans[piece]]
        pltpu.make_async_remote_copy(
            src_ref=spot, dst_ref=spot, send_sem=send_sem.at[0], recv_sem=sem.at[piece, r, c],
            device_id=device(dk=1), device_id_type=MESH).wait_recv()

    def relay(piece, at, order):
        take(piece, at, line_sem, k)
        pass_on(piece, at, order)

    keep = pltpu.make_async_copy(shard_ref, all_ref.at[row, col], own_sem)
    keep.start()
    pass_on(1, {}, "yzx")
    pass_on(0, {}, "zxy")
    for side in lines["y"]:
        relay(1, side, "zx")
    for up in lines["z"]:
        relay(0, up, "xy")
    for up in [{}] + lines["z"]:
        for across in lines["x"]:
            relay(0, up | across, "y")
        if up:
            for side in [{}] + lines["y"]:
                relay(1, up | side, "x")
    for up in [{}] + lines["z"]:
        for across in [{}] + lines["x"]:
            for side in lines["y"]:
                relay(0, up | across | side, "")
        for side in [{}] + lines["y"]:
            for across in lines["x"]:
                relay(1, up | across | side, "")
    for dz in range(nz):
        for dx in range(nx):
            for dy in range(ny):
                for piece in (0, 1):
                    take(piece, dict(dz=dz, dx=dx, dy=dy), pair_sem, 1 - k)
    keep.wait()
    for copy in sent:
        copy.wait_send()


def gather_all(shard):
    rows, cols = lax.axis_size("orow"), lax.axis_size("ocol")
    ny = cols // 2
    nx = ny if rows % ny == 0 else 1
    nz = rows // nx
    aux_local, span = shard.shape
    cut = aux_local * 5 // 9 // 16 * 16
    pushes = 2 * nz * nx * ny + (nz - 1) + nz * (nx - 1) + nz * nx * (ny - 1) + (ny - 1) + ny * (nz - 1) + nz * ny * (nx - 1)
    return pl.pallas_call(
        functools.partial(gather_kernel, nz, nx, ny, cut),
        out_shape=jax.ShapeDtypeStruct((rows, cols, aux_local, span), shard.dtype),
        in_specs=[pl.BlockSpec(memory_space=pltpu.VMEM)],
        out_specs=pl.BlockSpec(memory_space=pl.ANY),
        scratch_shapes=[
            pltpu.SemaphoreType.DMA,
            pltpu.SemaphoreType.DMA((pushes,)),
            pltpu.SemaphoreType.DMA((2, rows, ny)),
            pltpu.SemaphoreType.DMA((2, rows, ny)),
        ],
        compiler_params=pltpu.CompilerParams(collective_id=2, has_side_effects=True),
    )(shard)


def local(integrals, occ_count, occ_energy, vir_energy, task_iblock, task_jblock):
    aux_local, orbitals, virtuals = integrals.shape
    span = orbitals * virtuals
    blocks = lax.axis_size("orow")
    cols = lax.axis_size("ocol")
    row = lax.axis_index("orow")
    col = lax.axis_index("ocol")
    aux = aux_local * cols
    active = jnp.arange(orbitals) < occ_count[row]
    masked = integrals * active.astype(jnp.bfloat16)[None, :, None]
    shard = masked.reshape(aux_local, span)
    gathered = gather_all(shard).reshape(blocks, aux, span)
    i_list, j_list = task_iblock[:, 0], task_jblock
    ids = jnp.arange(blocks)
    i_hot = i_list[None, :] == ids[:, None]
    j_hot = j_list[None, :] == ids[:, None]
    first = jnp.sum((i_list == row)[None, :] & j_hot, axis=1).astype(jnp.int32)
    second = jnp.sum((j_list == row)[None, :] & i_hot, axis=1).astype(jnp.int32)
    numbers = jnp.concatenate([jnp.stack([row, col]).astype(jnp.int32), first + second, first])
    gamma, dens = pl.pallas_call(
        functools.partial(pair_kernel, orbitals, cols),
        grid_spec=pltpu.PrefetchScalarGridSpec(
            num_scalar_prefetch=2,
            grid=(blocks,),
            in_specs=[
                pl.BlockSpec((1, aux, span), lambda s, num, occ: (num[0], 0, 0)),
                pl.BlockSpec((1, aux, span), lambda s, num, occ: (s, 0, 0)),
                pl.BlockSpec((1, aux_local, span), lambda s, num, occ: (s, num[1], 0)),
                pl.BlockSpec((1, virtuals), lambda s, num, occ: (0, 0)),
                pl.BlockSpec((virtuals, 1), lambda s, num, occ: (0, 0)),
            ],
            out_specs=[
                pl.BlockSpec((aux_local, span), lambda s, num, occ: (0, 0)),
                pl.BlockSpec((virtuals // cols, virtuals), lambda s, num, occ: (0, 0)),
            ],
            scratch_shapes=[pltpu.VMEM((span, aux), jnp.bfloat16), pltpu.VMEM((virtuals, span), jnp.bfloat16)],
        ),
        out_shape=[
            jax.ShapeDtypeStruct((aux_local, span), jnp.float32),
            jax.ShapeDtypeStruct((virtuals // cols, virtuals), jnp.float32),
        ],
        compiler_params=pltpu.CompilerParams(vmem_limit_bytes=56 * 1024 * 1024),
    )(numbers, occ_energy, gathered, gathered, gathered, vir_energy[None, :], vir_energy[:, None])
    density = sum_density(dens, i_list.shape[0])
    return gamma.reshape(aux_local, orbitals, virtuals), density


def solution(mesh):
    return jax.shard_map(
        local,
        mesh=mesh,
        in_specs=(P("ocol", "orow", None), P(), P(), P(), P(), P()),
        out_specs=(P("ocol", "orow", None), P()),
        check_vma=False,
    )
```

```python
import functools

import jax
import jax.numpy as jnp
from jax import lax
from jax.experimental import pallas as pl
from jax.experimental.pallas import tpu as pltpu
from jax.sharding import PartitionSpec as P

MESH = pl.DeviceIdType.MESH


def pair_kernel(orbitals, cols, num_ref, occ_ref, gr_ref, gs_ref, gc_ref, vrow_ref, vcol_ref, gamma_ref, dens_ref, flip_ref, amp_ref):
    s = pl.program_id(0)
    blocks = pl.num_programs(0)
    row, col = num_ref[0], num_ref[1]
    virtuals = vrow_ref.shape[1]

    @pl.when(s == 0)
    def _():
        gamma_ref[...] = jnp.zeros_like(gamma_ref)
        dens_ref[...] = jnp.zeros_like(dens_ref)
        flip_ref[...] = gr_ref[0].T

    touch = num_ref[2 + s]
    first = num_ref[2 + blocks + s]

    @pl.when(touch > 0)
    def _():
        weight = touch.astype(jnp.float32)
        for i in range(orbitals):
            own = pl.ds(i * virtuals, virtuals)
            k_rows = jnp.dot(flip_ref[own, :], gs_ref[0], preferred_element_type=jnp.float32)
            parts = []
            for j in range(orbitals):
                k_ij = k_rows[:, j * virtuals:(j + 1) * virtuals]
                pair = occ_ref[row * orbitals + i] + occ_ref[s * orbitals + j]
                denominator = (pair - vcol_ref[...]) - vrow_ref[...]
                parts.append(((2.0 * k_ij - k_ij.T) / denominator).astype(jnp.bfloat16))
            amp = jnp.concatenate(parts, axis=1)
            amp_ref[i] = amp
            gamma_ref[:, own] += weight * lax.dot_general(
                gc_ref[0], amp, (((1,), (1,)), ((), ())), preferred_element_type=jnp.float32)

        @pl.when(first > 0)
        def _():
            strip = virtuals // cols
            count = first.astype(jnp.float32)
            for i in range(orbitals):
                mine = amp_ref[i, pl.ds(pl.multiple_of(col * strip, strip), strip), :]
                dens_ref[...] += count * lax.dot_general(
                    mine, amp_ref[i], (((1,), (1,)), ((), ())), preferred_element_type=jnp.float32)


def density_kernel(scale, part_ref, out_ref, arrived, send_sem, take_sem, pass_sem, row_sem, fan_sem, col_sem):
    rows, cols = lax.axis_size("orow"), lax.axis_size("ocol")
    row, col = lax.axis_index("orow"), lax.axis_index("ocol")
    barrier = pltpu.get_barrier_semaphore()

    def peer(step):
        return lax.rem(row + step, rows)

    def other(step):
        return lax.rem(col + step, cols)

    @pl.loop(1, rows)
    def _(step):
        pl.semaphore_signal(barrier, inc=1, device_id={"orow": peer(step)}, device_id_type=MESH)

    @pl.loop(1, cols)
    def _(step):
        pl.semaphore_signal(barrier, inc=1, device_id={"ocol": other(step)}, device_id_type=MESH)

    pl.semaphore_wait(barrier, rows + cols - 2)

    def scatter(step):
        return pltpu.make_async_remote_copy(
            src_ref=part_ref.at[peer(step)], dst_ref=arrived.at[step - 1], send_sem=send_sem.at[step - 1],
            recv_sem=take_sem.at[step - 1], device_id={"orow": peer(step)}, device_id_type=MESH)

    def spread(step):
        spot = out_ref.at[col, row]
        return pltpu.make_async_remote_copy(
            src_ref=spot, dst_ref=spot, send_sem=pass_sem.at[step - 1],
            recv_sem=row_sem.at[step - 1], device_id={"orow": peer(step)}, device_id_type=MESH)

    def fan(step):
        spot = out_ref.at[col]
        return pltpu.make_async_remote_copy(
            src_ref=spot, dst_ref=spot, send_sem=fan_sem.at[step - 1],
            recv_sem=col_sem.at[step - 1], device_id={"ocol": other(step)}, device_id_type=MESH)

    @pl.loop(1, rows)
    def _(step):
        scatter(step).start()

    total = part_ref[row]
    for step in range(1, rows):
        scatter(step).wait()
        total = total + arrived[step - 1]
    out_ref[col, row] = total * scale

    @pl.loop(1, rows)
    def _(step):
        spread(step).start()

    @pl.loop(1, rows)
    def _(step):
        spread(step).wait()

    @pl.loop(1, cols)
    def _(step):
        fan(step).start()

    @pl.loop(1, cols)
    def _(step):
        fan(step).wait()


def sum_density(part, tasks):
    rows, cols = lax.axis_size("orow"), lax.axis_size("ocol")
    strip, virtuals = part.shape
    share = strip // rows
    full = pl.pallas_call(
        functools.partial(density_kernel, 1.0 / tasks),
        out_shape=jax.ShapeDtypeStruct((cols, rows, share, virtuals), jnp.float32),
        in_specs=[pl.BlockSpec(memory_space=pltpu.VMEM)],
        out_specs=pl.BlockSpec(memory_space=pltpu.VMEM),
        scratch_shapes=[
            pltpu.VMEM((rows - 1, share, virtuals), jnp.float32),
            pltpu.SemaphoreType.DMA((rows - 1,)),
            pltpu.SemaphoreType.DMA((rows - 1,)),
            pltpu.SemaphoreType.DMA((rows - 1,)),
            pltpu.SemaphoreType.DMA((rows - 1,)),
            pltpu.SemaphoreType.DMA((cols - 1,)),
            pltpu.SemaphoreType.DMA((cols - 1,)),
        ],
        compiler_params=pltpu.CompilerParams(collective_id=1, has_side_effects=True),
    )(part.reshape(rows, share, virtuals))
    return full.reshape(virtuals, virtuals)


def gather_kernel(nz, nx, ny, cut, shard_ref, all_ref, own_sem, send_sem, line_sem, pair_sem):
    aux_local = shard_ref.shape[0]
    row, col = lax.axis_index("orow"), lax.axis_index("ocol")
    z, x, y, k = row // nx, lax.rem(row, nx), col // 2, lax.rem(col, 2)
    spans = (pl.ds(0, cut), pl.ds(cut, aux_local - cut))

    def turn(at, by, extent):
        return lax.rem(at + by, extent)

    def place(dz=0, dx=0, dy=0):
        return turn(z, dz, nz) * nx + turn(x, dx, nx), turn(y, dy, ny)

    def device(dz=0, dx=0, dy=0, dk=0):
        r, c = place(dz, dx, dy)
        return {"orow": r, "ocol": c * 2 + lax.rem(k + dk, 2)}

    near = sorted(range(1, nz), key=lambda d: min(d, nz - d))
    lines = {
        "z": [dict(dz=d) for d in near],
        "x": [dict(dx=d) for d in range(1, nx)],
        "y": [dict(dy=d) for d in range(1, ny)],
    }
    peers = lines["z"] + lines["x"] + lines["y"] + [dict(dk=1)]
    barrier = pltpu.get_barrier_semaphore()
    for peer in peers:
        pl.semaphore_signal(barrier, inc=1, device_id=device(**peer), device_id_type=MESH)
    pl.semaphore_wait(barrier, len(peers))

    sent = []

    def push(piece, at, source, sem, peer):
        r, c = place(**at)
        copy = pltpu.make_async_remote_copy(
            src_ref=source, dst_ref=all_ref.at[r, c * 2 + k, spans[piece]], send_sem=send_sem.at[len(sent)],
            recv_sem=sem, device_id=device(**peer), device_id_type=MESH)
        copy.start()
        sent.append(copy)

    def pass_on(piece, at, order):
        r, c = place(**at)
        own = not at
        source = shard_ref.at[spans[piece]] if own else all_ref.at[r, c * 2 + k, spans[piece]]
        for axis in order:
            for peer in lines[axis]:
                push(piece, at, source, line_sem.at[piece, r, c], peer)
        push(piece, at, source, pair_sem.at[piece, r, c], dict(dk=1))

    def take(piece, at, sem, core):
        r, c = place(**at)
        spot = all_ref.at[r, c * 2 + core, spans[piece]]
        pltpu.make_async_remote_copy(
            src_ref=spot, dst_ref=spot, send_sem=send_sem.at[0], recv_sem=sem.at[piece, r, c],
            device_id=device(dk=1), device_id_type=MESH).wait_recv()

    def relay(piece, at, order):
        take(piece, at, line_sem, k)
        pass_on(piece, at, order)

    keep = pltpu.make_async_copy(shard_ref, all_ref.at[row, col], own_sem)
    keep.start()
    pass_on(1, {}, "yzx")
    pass_on(0, {}, "zxy")
    for side in lines["y"]:
        relay(1, side, "zx")
    for up in lines["z"]:
        relay(0, up, "xy")
    for up in [{}] + lines["z"]:
        for across in lines["x"]:
            relay(0, up | across, "y")
        if up:
            for side in [{}] + lines["y"]:
                relay(1, up | side, "x")
    for up in [{}] + lines["z"]:
        for across in [{}] + lines["x"]:
            for side in lines["y"]:
                relay(0, up | across | side, "")
        for side in [{}] + lines["y"]:
            for across in lines["x"]:
                relay(1, up | across | side, "")
    for dz in range(nz):
        for dx in range(nx):
            for dy in range(ny):
                for piece in (0, 1):
                    take(piece, dict(dz=dz, dx=dx, dy=dy), pair_sem, 1 - k)
    keep.wait()
    for copy in sent:
        copy.wait_send()


def gather_all(shard):
    rows, cols = lax.axis_size("orow"), lax.axis_size("ocol")
    ny = cols // 2
    nx = ny if rows % ny == 0 else 1
    nz = rows // nx
    aux_local, span = shard.shape
    cut = aux_local * 7 // 11 // 16 * 16
    pushes = 2 * nz * nx * ny + (nz - 1) + nz * (nx - 1) + nz * nx * (ny - 1) + (ny - 1) + ny * (nz - 1) + nz * ny * (nx - 1)
    return pl.pallas_call(
        functools.partial(gather_kernel, nz, nx, ny, cut),
        out_shape=jax.ShapeDtypeStruct((rows, cols, aux_local, span), shard.dtype),
        in_specs=[pl.BlockSpec(memory_space=pltpu.VMEM)],
        out_specs=pl.BlockSpec(memory_space=pl.ANY),
        scratch_shapes=[
            pltpu.SemaphoreType.DMA,
            pltpu.SemaphoreType.DMA((pushes,)),
            pltpu.SemaphoreType.DMA((2, rows, ny)),
            pltpu.SemaphoreType.DMA((2, rows, ny)),
        ],
        compiler_params=pltpu.CompilerParams(collective_id=2, has_side_effects=True),
    )(shard)


def local(integrals, occ_count, occ_energy, vir_energy, task_iblock, task_jblock):
    aux_local, orbitals, virtuals = integrals.shape
    span = orbitals * virtuals
    blocks = lax.axis_size("orow")
    cols = lax.axis_size("ocol")
    row = lax.axis_index("orow")
    col = lax.axis_index("ocol")
    aux = aux_local * cols
    active = jnp.arange(orbitals) < occ_count[row]
    masked = integrals * active.astype(jnp.bfloat16)[None, :, None]
    shard = masked.reshape(aux_local, span)
    gathered = gather_all(shard).reshape(blocks, aux, span)
    i_list, j_list = task_iblock[:, 0], task_jblock
    ids = jnp.arange(blocks)
    i_hot = i_list[None, :] == ids[:, None]
    j_hot = j_list[None, :] == ids[:, None]
    first = jnp.sum((i_list == row)[None, :] & j_hot, axis=1).astype(jnp.int32)
    second = jnp.sum((j_list == row)[None, :] & i_hot, axis=1).astype(jnp.int32)
    numbers = jnp.concatenate([jnp.stack([row, col]).astype(jnp.int32), first + second, first])
    gamma, dens = pl.pallas_call(
        functools.partial(pair_kernel, orbitals, cols),
        grid_spec=pltpu.PrefetchScalarGridSpec(
            num_scalar_prefetch=2,
            grid=(blocks,),
            in_specs=[
                pl.BlockSpec((1, aux, span), lambda s, num, occ: (num[0], 0, 0)),
                pl.BlockSpec((1, aux, span), lambda s, num, occ: (s, 0, 0)),
                pl.BlockSpec((1, aux_local, span), lambda s, num, occ: (s, num[1], 0)),
                pl.BlockSpec((1, virtuals), lambda s, num, occ: (0, 0)),
                pl.BlockSpec((virtuals, 1), lambda s, num, occ: (0, 0)),
            ],
            out_specs=[
                pl.BlockSpec((aux_local, span), lambda s, num, occ: (0, 0)),
                pl.BlockSpec((virtuals // cols, virtuals), lambda s, num, occ: (0, 0)),
            ],
            scratch_shapes=[pltpu.VMEM((span, aux), jnp.bfloat16), pltpu.VMEM((orbitals, virtuals, span), jnp.bfloat16)],
        ),
        out_shape=[
            jax.ShapeDtypeStruct((aux_local, span), jnp.float32),
            jax.ShapeDtypeStruct((virtuals // cols, virtuals), jnp.float32),
        ],
        compiler_params=pltpu.CompilerParams(vmem_limit_bytes=56 * 1024 * 1024),
    )(numbers, occ_energy, gathered, gathered, gathered, vir_energy[None, :], vir_energy[:, None])
    density = sum_density(dens, i_list.shape[0])
    return gamma.reshape(aux_local, orbitals, virtuals), density


def solution(mesh):
    return jax.shard_map(
        local,
        mesh=mesh,
        in_specs=(P("ocol", "orow", None), P(), P(), P(), P(), P()),
        out_specs=(P("ocol", "orow", None), P()),
        check_vma=False,
    )
```

```python
import functools

import jax
import jax.numpy as jnp
from jax import lax
from jax.experimental import pallas as pl
from jax.experimental.pallas import tpu as pltpu
from jax.sharding import PartitionSpec as P

MESH = pl.DeviceIdType.MESH


def pair_kernel(orbitals, cols, num_ref, occ_ref, gr_ref, gs_ref, gc_ref, vrow_ref, vcol_ref, gamma_ref, dens_ref, flip_ref, amp_ref):
    s = pl.program_id(0)
    blocks = pl.num_programs(0)
    row, col = num_ref[0], num_ref[1]
    virtuals = vrow_ref.shape[1]

    @pl.when(s == 0)
    def _():
        gamma_ref[...] = jnp.zeros_like(gamma_ref)
        dens_ref[...] = jnp.zeros_like(dens_ref)
        flip_ref[...] = gr_ref[0].T

    touch = num_ref[2 + s]
    first = num_ref[2 + blocks + s]

    @pl.when(touch > 0)
    def _():
        weight = touch.astype(jnp.float32)
        for i in range(orbitals):
            own = pl.ds(i * virtuals, virtuals)
            k_rows = jnp.dot(flip_ref[own, :], gs_ref[0], preferred_element_type=jnp.float32)
            parts = []
            for j in range(orbitals):
                k_ij = k_rows[:, j * virtuals:(j + 1) * virtuals]
                pair = occ_ref[row * orbitals + i] + occ_ref[s * orbitals + j]
                denominator = (pair - vcol_ref[...]) - vrow_ref[...]
                parts.append(((2.0 * k_ij - k_ij.T) / denominator).astype(jnp.bfloat16))
            amp = jnp.concatenate(parts, axis=1)
            amp_ref[i] = amp
            gamma_ref[:, own] += weight * lax.dot_general(
                gc_ref[0], amp, (((1,), (1,)), ((), ())), preferred_element_type=jnp.float32)

        @pl.when(first > 0)
        def _():
            strip = virtuals // cols
            count = first.astype(jnp.float32)
            for i in range(orbitals):
                mine = amp_ref[i, pl.ds(pl.multiple_of(col * strip, strip), strip), :]
                dens_ref[...] += count * lax.dot_general(
                    mine, amp_ref[i], (((1,), (1,)), ((), ())), preferred_element_type=jnp.float32)


def density_kernel(scale, part_ref, out_ref, arrived, send_sem, take_sem, pass_sem, row_sem, fan_sem, col_sem):
    rows, cols = lax.axis_size("orow"), lax.axis_size("ocol")
    row, col = lax.axis_index("orow"), lax.axis_index("ocol")
    barrier = pltpu.get_barrier_semaphore()

    def peer(step):
        return lax.rem(row + step, rows)

    def other(step):
        return lax.rem(col + step, cols)

    @pl.loop(1, rows)
    def _(step):
        pl.semaphore_signal(barrier, inc=1, device_id={"orow": peer(step)}, device_id_type=MESH)

    @pl.loop(1, cols)
    def _(step):
        pl.semaphore_signal(barrier, inc=1, device_id={"ocol": other(step)}, device_id_type=MESH)

    pl.semaphore_wait(barrier, rows + cols - 2)

    def scatter(step):
        return pltpu.make_async_remote_copy(
            src_ref=part_ref.at[peer(step)], dst_ref=arrived.at[step - 1], send_sem=send_sem.at[step - 1],
            recv_sem=take_sem.at[step - 1], device_id={"orow": peer(step)}, device_id_type=MESH)

    def spread(step):
        spot = out_ref.at[col, row]
        return pltpu.make_async_remote_copy(
            src_ref=spot, dst_ref=spot, send_sem=pass_sem.at[step - 1],
            recv_sem=row_sem.at[step - 1], device_id={"orow": peer(step)}, device_id_type=MESH)

    def fan(step):
        spot = out_ref.at[col]
        return pltpu.make_async_remote_copy(
            src_ref=spot, dst_ref=spot, send_sem=fan_sem.at[step - 1],
            recv_sem=col_sem.at[step - 1], device_id={"ocol": other(step)}, device_id_type=MESH)

    @pl.loop(1, rows)
    def _(step):
        scatter(step).start()

    total = part_ref[row]
    for step in range(1, rows):
        scatter(step).wait()
        total = total + arrived[step - 1]
    out_ref[col, row] = total * scale

    @pl.loop(1, rows)
    def _(step):
        spread(step).start()

    @pl.loop(1, rows)
    def _(step):
        spread(step).wait()

    @pl.loop(1, cols)
    def _(step):
        fan(step).start()

    @pl.loop(1, cols)
    def _(step):
        fan(step).wait()


def sum_density(part, tasks):
    rows, cols = lax.axis_size("orow"), lax.axis_size("ocol")
    strip, virtuals = part.shape
    share = strip // rows
    full = pl.pallas_call(
        functools.partial(density_kernel, 1.0 / tasks),
        out_shape=jax.ShapeDtypeStruct((cols, rows, share, virtuals), jnp.float32),
        in_specs=[pl.BlockSpec(memory_space=pltpu.VMEM)],
        out_specs=pl.BlockSpec(memory_space=pltpu.VMEM),
        scratch_shapes=[
            pltpu.VMEM((rows - 1, share, virtuals), jnp.float32),
            pltpu.SemaphoreType.DMA((rows - 1,)),
            pltpu.SemaphoreType.DMA((rows - 1,)),
            pltpu.SemaphoreType.DMA((rows - 1,)),
            pltpu.SemaphoreType.DMA((rows - 1,)),
            pltpu.SemaphoreType.DMA((cols - 1,)),
            pltpu.SemaphoreType.DMA((cols - 1,)),
        ],
        compiler_params=pltpu.CompilerParams(collective_id=1, has_side_effects=True),
    )(part.reshape(rows, share, virtuals))
    return full.reshape(virtuals, virtuals)


def gather_kernel(nz, nx, ny, cut, shard_ref, all_ref, own_sem, send_sem, line_sem, pair_sem):
    aux_local = shard_ref.shape[0]
    row, col = lax.axis_index("orow"), lax.axis_index("ocol")
    z, x, y, k = row // nx, lax.rem(row, nx), col // 2, lax.rem(col, 2)
    spans = (pl.ds(0, cut), pl.ds(cut, aux_local - cut))

    def turn(at, by, extent):
        return lax.rem(at + by, extent)

    def place(dz=0, dx=0, dy=0):
        return turn(z, dz, nz) * nx + turn(x, dx, nx), turn(y, dy, ny)

    def device(dz=0, dx=0, dy=0, dk=0):
        r, c = place(dz, dx, dy)
        return {"orow": r, "ocol": c * 2 + lax.rem(k + dk, 2)}

    near = sorted(range(1, nz), key=lambda d: min(d, nz - d))
    lines = {
        "z": [dict(dz=d) for d in near],
        "x": [dict(dx=d) for d in range(1, nx)],
        "y": [dict(dy=d) for d in range(1, ny)],
    }
    peers = lines["z"] + lines["x"] + lines["y"] + [dict(dk=1)]
    barrier = pltpu.get_barrier_semaphore()
    for peer in peers:
        pl.semaphore_signal(barrier, inc=1, device_id=device(**peer), device_id_type=MESH)
    pl.semaphore_wait(barrier, len(peers))

    sent = []

    def push(piece, at, source, sem, peer):
        r, c = place(**at)
        copy = pltpu.make_async_remote_copy(
            src_ref=source, dst_ref=all_ref.at[r, c * 2 + k, spans[piece]], send_sem=send_sem.at[len(sent)],
            recv_sem=sem, device_id=device(**peer), device_id_type=MESH)
        copy.start()
        sent.append(copy)

    def pass_on(piece, at, order):
        r, c = place(**at)
        own = not at
        source = shard_ref.at[spans[piece]] if own else all_ref.at[r, c * 2 + k, spans[piece]]
        for axis in order:
            for peer in lines[axis]:
                push(piece, at, source, line_sem.at[piece, r, c], peer)
        push(piece, at, source, pair_sem.at[piece, r, c], dict(dk=1))

    def take(piece, at, sem, core):
        r, c = place(**at)
        spot = all_ref.at[r, c * 2 + core, spans[piece]]
        pltpu.make_async_remote_copy(
            src_ref=spot, dst_ref=spot, send_sem=send_sem.at[0], recv_sem=sem.at[piece, r, c],
            device_id=device(dk=1), device_id_type=MESH).wait_recv()

    def relay(piece, at, order):
        take(piece, at, line_sem, k)
        pass_on(piece, at, order)

    keep = pltpu.make_async_copy(shard_ref, all_ref.at[row, col], own_sem)
    keep.start()
    pass_on(1, {}, "yzx")
    pass_on(0, {}, "zxy")
    for side in lines["y"]:
        relay(1, side, "zx")
    for up in lines["z"]:
        relay(0, up, "xy")
    for up in [{}] + lines["z"]:
        for across in lines["x"]:
            relay(0, up | across, "y")
        if up:
            for side in [{}] + lines["y"]:
                relay(1, up | side, "x")
    for up in [{}] + lines["z"]:
        for across in [{}] + lines["x"]:
            for side in lines["y"]:
                relay(0, up | across | side, "")
        for side in [{}] + lines["y"]:
            for across in lines["x"]:
                relay(1, up | across | side, "")
    for dz in range(nz):
        for dx in range(nx):
            for dy in range(ny):
                for piece in (0, 1):
                    take(piece, dict(dz=dz, dx=dx, dy=dy), pair_sem, 1 - k)
    keep.wait()
    for copy in sent:
        copy.wait_send()


def gather_all(shard):
    rows, cols = lax.axis_size("orow"), lax.axis_size("ocol")
    ny = cols // 2
    nx = ny if rows % ny == 0 else 1
    nz = rows // nx
    aux_local, span = shard.shape
    cut = aux_local * 2 // 3 // 16 * 16
    pushes = 2 * nz * nx * ny + (nz - 1) + nz * (nx - 1) + nz * nx * (ny - 1) + (ny - 1) + ny * (nz - 1) + nz * ny * (nx - 1)
    return pl.pallas_call(
        functools.partial(gather_kernel, nz, nx, ny, cut),
        out_shape=jax.ShapeDtypeStruct((rows, cols, aux_local, span), shard.dtype),
        in_specs=[pl.BlockSpec(memory_space=pltpu.VMEM)],
        out_specs=pl.BlockSpec(memory_space=pl.ANY),
        scratch_shapes=[
            pltpu.SemaphoreType.DMA,
            pltpu.SemaphoreType.DMA((pushes,)),
            pltpu.SemaphoreType.DMA((2, rows, ny)),
            pltpu.SemaphoreType.DMA((2, rows, ny)),
        ],
        compiler_params=pltpu.CompilerParams(collective_id=2, has_side_effects=True),
    )(shard)


def local(integrals, occ_count, occ_energy, vir_energy, task_iblock, task_jblock):
    aux_local, orbitals, virtuals = integrals.shape
    span = orbitals * virtuals
    blocks = lax.axis_size("orow")
    cols = lax.axis_size("ocol")
    row = lax.axis_index("orow")
    col = lax.axis_index("ocol")
    aux = aux_local * cols
    active = jnp.arange(orbitals) < occ_count[row]
    masked = integrals * active.astype(jnp.bfloat16)[None, :, None]
    shard = masked.reshape(aux_local, span)
    gathered = gather_all(shard).reshape(blocks, aux, span)
    i_list, j_list = task_iblock[:, 0], task_jblock
    ids = jnp.arange(blocks)
    i_hot = i_list[None, :] == ids[:, None]
    j_hot = j_list[None, :] == ids[:, None]
    first = jnp.sum((i_list == row)[None, :] & j_hot, axis=1).astype(jnp.int32)
    second = jnp.sum((j_list == row)[None, :] & i_hot, axis=1).astype(jnp.int32)
    numbers = jnp.concatenate([jnp.stack([row, col]).astype(jnp.int32), first + second, first])
    gamma, dens = pl.pallas_call(
        functools.partial(pair_kernel, orbitals, cols),
        grid_spec=pltpu.PrefetchScalarGridSpec(
            num_scalar_prefetch=2,
            grid=(blocks,),
            in_specs=[
                pl.BlockSpec((1, aux, span), lambda s, num, occ: (num[0], 0, 0)),
                pl.BlockSpec((1, aux, span), lambda s, num, occ: (s, 0, 0)),
                pl.BlockSpec((1, aux_local, span), lambda s, num, occ: (s, num[1], 0)),
                pl.BlockSpec((1, virtuals), lambda s, num, occ: (0, 0)),
                pl.BlockSpec((virtuals, 1), lambda s, num, occ: (0, 0)),
            ],
            out_specs=[
                pl.BlockSpec((aux_local, span), lambda s, num, occ: (0, 0)),
                pl.BlockSpec((virtuals // cols, virtuals), lambda s, num, occ: (0, 0)),
            ],
            scratch_shapes=[pltpu.VMEM((span, aux), jnp.bfloat16), pltpu.VMEM((orbitals, virtuals, span), jnp.bfloat16)],
        ),
        out_shape=[
            jax.ShapeDtypeStruct((aux_local, span), jnp.float32),
            jax.ShapeDtypeStruct((virtuals // cols, virtuals), jnp.float32),
        ],
        compiler_params=pltpu.CompilerParams(vmem_limit_bytes=56 * 1024 * 1024),
    )(numbers, occ_energy, gathered, gathered, gathered, vir_energy[None, :], vir_energy[:, None])
    density = sum_density(dens, i_list.shape[0])
    return gamma.reshape(aux_local, orbitals, virtuals), density


def solution(mesh):
    return jax.shard_map(
        local,
        mesh=mesh,
        in_specs=(P("ocol", "orow", None), P(), P(), P(), P(), P()),
        out_specs=(P("ocol", "orow", None), P()),
        check_vma=False,
    )
```
